32 devices in a mesh: groups: 2 (over y), ctx: 4 (over z), head: 2 (over x), tp: 2 (over core).
Axes of the slice: x: 2, y: 2, z: 4, core: 2. Of those that a mesh axis runs over, the one named last changes fastest.
Arguments:
- queries: bfloat16 [32, 2048, 128], P(('head', 'tp'), ('groups', 'ctx')), parts along dimension 1, may hold values from -80 to 80
- stretch_keys: bfloat16 [8, 2048, 128], P(('head', 'tp'), ('groups', 'ctx')), parts along dimension 1, may hold values from -120 to 120
- stretch_values: bfloat16 [8, 2048, 128], P(('head', 'tp'), ('groups', 'ctx')), parts along dimension 1, may hold values from -6 to 6
- cache_keys: bfloat16 [8, 32768, 128], P(('head', 'tp'), ('groups', 'ctx')), parts along dimension 1, may hold values from -6 to 6
- cache_values: bfloat16 [8, 32768, 128], P(('head', 'tp'), ('groups', 'ctx')), parts along dimension 1, may hold values from -6 to 6
- block_picks: int32 [4, 8, 16], P('groups'), parts along dimension 0, may hold values from 0 to 31, as said below
- block_table: int32 [64], P('groups'), parts along dimension 0, may hold values from 0 to 31, as said below
Outputs:
- attended: bfloat16 [32, 2048, 128], P(('head', 'tp'), ('groups', 'ctx')), parts along dimension 1
The draws below stay inside these ranges and needn't reach their ends.
There are 2 independent parts, one for each index of `groups`. The reference program is written for one: setup_inputs(seed, part) draws one part's arguments, and reference() takes and returns one part's arrays. A program takes and returns all parts, laid end to end along the dimension named above; each array names one. Nothing has to cross between parts.
Inputs may be any that keep to these rules, and one draw needn't show every extreme that they name: `block_picks`: for each query block and KV head the 16 picks are different logical blocks; exactly 4 of them have slots on each of 4 different indices of ctx, slot s lying on index s // 8. `block_table`: A permutation of the 32 physical slots.
All inputs are finite; a program needn't handle non-finite values.
Results may differ from the reference program's by a relative error of at most 0.0032.
Values may be sent and summed in bfloat16 or wider, within the bound.
No kernel may reach another device: no remote copies, remote signals or barrier semaphores. Data moves between devices by JAX's collectives and lax.ppermute only.
A program may use at most 64 MiB of HBM per device.

```python
import jax
import jax.numpy as jnp
from jax import lax

QH = 32
KVH = 8
HD = 128
BLOCK = 512
TOPK = 16
NBLK_DEV = 8
TOK_DEV = 256
STRETCH = 1024
QBLK = 2
CACHE_BLOCKS = 32
CAP = 4
OWNERS = 4


def query_key_pair(key):
    base = jax.random.fold_in(key, 31)
    key_q, key_k = jax.random.split(base, 2)
    queries = 2.5 * jax.random.normal(key_q, (QH, STRETCH, HD), jnp.float32)
    keys_out = jax.random.normal(key_k, (KVH, STRETCH, HD), jnp.float32)
    return (queries, keys_out)


def draw_queries(key, part):
    return query_key_pair(key)[0].astype(jnp.bfloat16)


def draw_stretch_keys(key, part):
    return query_key_pair(key)[1].astype(jnp.bfloat16)


def block_layout(key):
    base = jax.random.fold_in(key, 53)
    key_t, key_h, key_s, key_l = jax.random.split(base, 4)
    prior_token_total = CACHE_BLOCKS // NBLK_DEV
    table = jax.random.permutation(key_t, CACHE_BLOCKS).astype(jnp.int32)
    inverse = jnp.argsort(table).astype(jnp.int32)
    preferred_worker_index = jax.random.permutation(key_h, prior_token_total)
    relevance_increment = jnp.where(preferred_worker_index < max(1, prior_token_total // 8), 3000, 0).astype(jnp.int32)
    noise_perturbation = jax.random.randint(key_s, (QBLK, KVH, prior_token_total), 0, 4000, jnp.int32)
    tile_relevance = (noise_perturbation + relevance_increment[None, None, :]) * prior_token_total + jnp.arange(prior_token_total, dtype=jnp.int32)
    owners = jnp.argsort(-tile_relevance, axis=-1)[..., :OWNERS].astype(jnp.int32)
    starting = jax.random.randint(key_l, (QBLK, KVH, OWNERS, 1), 0, NBLK_DEV, jnp.int32)
    in_owner = (starting + jnp.arange(CAP, dtype=jnp.int32)) % NBLK_DEV
    physical = (owners[..., None] * NBLK_DEV + in_owner).reshape(QBLK, KVH, TOPK)
    return (table, inverse[physical].astype(jnp.int32))


def draw_block_picks(key, part):
    return block_layout(key)[1]


def draw_block_table(key, part):
    return block_layout(key)[0]


def shard_levels(own_key, shape, pieces, smallest, high):
    def one(position, parts):
        draws = jax.random.uniform(jax.random.fold_in(jax.random.fold_in(own_key, 6), position), (parts,), jnp.float32, smallest / len(pieces), high / len(pieces))
        return jnp.repeat(jnp.exp(draws), shape[position] // parts).reshape((-1,) + (1,) * (len(shape) - position - 1))

    factor_of = one(*pieces[0])
    for cut in pieces[1:]:
        factor_of = factor_of * one(*cut)
    return factor_of


def scatter_about(key, extent, width, reach, shards=(), kind=jnp.bfloat16):
    values = jax.random.normal(key, extent, jnp.float32) * width
    if len(shards) > 0:
        values = shard_levels(key, extent, shards, -0.22, 0.18) * values
    return jnp.clip(values, min=-reach, max=reach).astype(kind)


def setup_inputs(seed: int = 0, part: int = 0) -> dict:
    arg_keys = jax.random.split(jax.random.key(seed), 8)
    part_keys = jax.random.split(jax.random.fold_in(arg_keys[7], part), 8)
    return {
        "queries": draw_queries(jax.random.fold_in(jax.random.fold_in(arg_keys[7], part), 71), part),
        "stretch_keys": draw_stretch_keys(jax.random.fold_in(jax.random.fold_in(arg_keys[7], part), 71), part),
        "stretch_values": scatter_about(part_keys[2], (KVH, STRETCH, HD), 1.0, 6.0, ((0, 4), (1, 4))),
        "cache_keys": scatter_about(part_keys[3], (KVH, CACHE_BLOCKS * BLOCK, HD), 1.0, 6.0, ((0, 4), (1, 4))),
        "cache_values": scatter_about(part_keys[4], (KVH, CACHE_BLOCKS * BLOCK, HD), 1.0, 6.0, ((0, 4), (1, 4))),
        "block_picks": draw_block_picks(jax.random.fold_in(jax.random.fold_in(arg_keys[7], part), 71), part),
        "block_table": draw_block_table(jax.random.fold_in(jax.random.fold_in(arg_keys[7], part), 71), part),
    }


def reference(queries, stretch_keys, stretch_values, cache_keys, cache_values, block_picks, block_table):
    q_per_kv = QH // KVH
    tiled_keyset = cache_keys.reshape(KVH, CACHE_BLOCKS, BLOCK, HD)
    value_blocks = cache_values.reshape(KVH, CACHE_BLOCKS, BLOCK, HD)
    padded_keys = jnp.pad(stretch_keys, ((0, 0), (TOK_DEV, 0), (0, 0)))
    padded_values = jnp.pad(stretch_values, ((0, 0), (TOK_DEV, 0), (0, 0)))
    head_ids = jnp.arange(KVH, dtype=jnp.int32)[:, None]
    span_cols = TOPK * BLOCK
    columns = jnp.arange(span_cols + BLOCK + TOK_DEV, dtype=jnp.int32)
    positions = jnp.arange(BLOCK, dtype=jnp.int32)
    relative = columns[None, :] - span_cols

    def one_block(block_id):
        first_row = (block_id * BLOCK).astype(jnp.int32)
        allowed_mask = (columns[None, :] < span_cols) | ((relative <= positions[:, None] + TOK_DEV) & (relative > positions[:, None]) & (relative >= TOK_DEV - first_row))
        q_block = lax.dynamic_slice_in_dim(queries, first_row, BLOCK, 1)
        q_block = q_block.reshape(KVH, q_per_kv, BLOCK, HD).astype(jnp.float32)
        window_keys = lax.dynamic_slice_in_dim(padded_keys, first_row, BLOCK + TOK_DEV, 1)
        window_values = lax.dynamic_slice_in_dim(padded_values, first_row, BLOCK + TOK_DEV, 1)
        physical = block_table[block_picks[block_id]].astype(jnp.int32)
        selected_keyset = tiled_keyset[head_ids, physical].reshape(KVH, span_cols, HD)
        picked_values = value_blocks[head_ids, physical].reshape(KVH, span_cols, HD)
        all_keys = jnp.concatenate([selected_keyset, window_keys], axis=1).astype(jnp.float32)
        all_values = jnp.concatenate([picked_values, window_values], axis=1).astype(jnp.float32)
        tile_relevance = jnp.einsum("gqrd,gkd->gqrk", q_block, all_keys) * (HD ** -0.5)
        tile_relevance = jnp.where(allowed_mask[None, None], tile_relevance, -jnp.inf)
        row_max = jnp.max(tile_relevance, axis=-1, keepdims=True)
        weights = jnp.exp(tile_relevance - row_max)
        row_sum = jnp.sum(weights, axis=-1, keepdims=True)
        rounded = lax.optimization_barrier(weights.astype(jnp.bfloat16)).astype(jnp.float32)
        mixed = jnp.einsum("gqrk,gkd->gqrd", rounded, all_values) / row_sum
        return mixed.reshape(QH, BLOCK, HD).astype(jnp.bfloat16)

    result = lax.map(one_block, jnp.arange(QBLK, dtype=jnp.int32))
    return jnp.transpose(result, (1, 0, 2, 3)).reshape(QH, STRETCH, HD)
```

```python
import functools

import jax
import jax.numpy as jnp
import numpy as np
from jax import lax
from jax.experimental import pallas as pl
from jax.experimental.pallas import tpu as pltpu
from jax.sharding import PartitionSpec as P

BLOCK = 512
TOPK = 16


def shifted(value, axis, by):
    count = lax.axis_size(axis)
    pairs = [(i, i + by) for i in range(count) if 0 <= i + by < count]
    return lax.ppermute(value, axis, pairs)


def as_sent(value):

    def short(part):
        return part.astype(jnp.bfloat16) if part.dtype == jnp.float32 else part

    return jax.tree.map(short, value)


def partner(value, axis, bit):
    mask = 2**bit
    pairs = [(source, source ^ mask) for source in range(lax.axis_size(axis))]
    return lax.ppermute(value, axis, pairs)


def lookup(lookup_table, indices):
    entries = jnp.arange(lookup_table.shape[0], dtype=jnp.int32)
    return jnp.sum(jnp.where(indices[..., None] == entries, lookup_table, 0), axis=-1)


def owner_rank(owners):
    ordinal = jnp.arange(owners.shape[-1], dtype=jnp.int32)
    before = (owners[..., :, None] == owners[..., None, :]) & (ordinal[None, :] < ordinal[:, None])
    return jnp.sum(before, axis=-1)


def pick_rows(source, indices):
    return source[indices]


def take_blocks(blocks, indices):
    return jax.vmap(pick_rows)(blocks, indices)


def attend(query_rows, all_keys, all_values, allowed_mask):
    tile_relevance = jnp.einsum(
        "rd,kd->rk", query_rows, all_keys, preferred_element_type=jnp.float32
    )
    tile_relevance = tile_relevance * query_rows.shape[-1] ** (-0.5)
    tile_relevance = jnp.where(allowed_mask, tile_relevance, -jnp.inf)
    row_max = jnp.max(tile_relevance, axis=-1, keepdims=True)
    weights = jnp.exp(tile_relevance - row_max)
    weight_sum = jnp.sum(weights, axis=-1, keepdims=True)
    mixed = jnp.einsum(
        "rk,kd->rd", weights.astype(jnp.bfloat16), all_values, preferred_element_type=jnp.float32
    )
    return (mixed / weight_sum).astype(jnp.bfloat16)


def moved_blocks(
    queries, stretch_keys, stretch_values, cache_keys, cache_values, block_picks, block_table
):
    kv_dev, tok_dev, head_dim = stretch_keys.shape
    q_per_kv = queries.shape[0] // kv_dev
    blocks_dev = cache_keys.shape[1] // BLOCK
    ctx_size = lax.axis_size("ctx")
    ctx_index = lax.axis_index("ctx")
    per_peer = max(1, TOPK // ctx_size)
    parity = ctx_index % 2
    head_ids = lax.axis_index(("head", "tp")) * kv_dev + jnp.arange(kv_dev, dtype=jnp.int32)
    selector = head_ids[:, None] == jnp.arange(block_picks.shape[1], dtype=jnp.int32)[None, :]
    my_picks = jnp.sum(jnp.where(selector[None, :, :, None], block_picks[:, None, :, :], 0), axis=2)
    physical = lookup(block_table, my_picks)
    owners = physical // blocks_dev
    in_owner = physical % blocks_dev
    peer_rank = owner_rank(owners)
    targets = np.arange(ctx_size) * tok_dev // BLOCK
    target_owner = owners[targets]
    target_rank = peer_rank[targets]
    target_local = in_owner[targets]
    slot_ids = jnp.arange(per_peer, dtype=jnp.int32)
    matched = (target_owner[:, :, None, :] == ctx_index) & (
        target_rank[:, :, None, :] == slot_ids[None, None, :, None]
    )
    chosen = jnp.sum(jnp.where(matched, target_local[:, :, None, :], 0), axis=-1)
    usable = jnp.any(matched, axis=-1)
    chosen = jnp.transpose(chosen, (1, 0, 2)).reshape(kv_dev, ctx_size * per_peer)
    usable = jnp.transpose(usable, (1, 0, 2)).reshape(kv_dev, ctx_size * per_peer)
    my_block = ctx_index * tok_dev // BLOCK
    my_owner = lax.dynamic_index_in_dim(owners, my_block, 0, keepdims=False)
    my_rank = lax.dynamic_index_in_dim(peer_rank, my_block, 0, keepdims=False)
    my_slot = my_owner * per_peer + my_rank
    prev_keys, prev_values = shifted((stretch_keys, stretch_values), "ctx", 1)
    half_rows = BLOCK // 2
    key_halves = cache_keys.reshape(kv_dev, blocks_dev * 2, half_rows, head_dim)
    value_halves = cache_values.reshape(kv_dev, blocks_dev * 2, half_rows, head_dim)
    row_side = jnp.asarray(np.repeat(np.arange(ctx_size) % 2, per_peer), jnp.int32)
    half_index = chosen * 2 + row_side[None, :]
    sent_keys = jnp.where(usable[:, :, None, None], take_blocks(key_halves, half_index), 0).astype(
        jnp.bfloat16
    )
    sent_values = jnp.where(
        usable[:, :, None, None], take_blocks(value_halves, half_index), 0
    ).astype(jnp.bfloat16)
    got_keys, got_values = (
        lax.all_to_all(sent_keys, "ctx", split_axis=1, concat_axis=1, tiled=True),
        lax.all_to_all(sent_values, "ctx", split_axis=1, concat_axis=1, tiled=True),
    )
    mine_keys = take_blocks(got_keys, my_slot)
    mine_values = take_blocks(got_values, my_slot)
    other_keys, other_values = (
        partner(as_sent(mine_keys), "ctx", 0).astype(mine_keys.dtype),
        partner(as_sent(mine_values), "ctx", 0).astype(mine_values.dtype),
    )
    first_keys = jnp.where(parity == 0, mine_keys, other_keys)
    second_keys = jnp.where(parity == 0, other_keys, mine_keys)
    first_values = jnp.where(parity == 0, mine_values, other_values)
    second_values = jnp.where(parity == 0, other_values, mine_values)
    live_keys = jnp.concatenate([first_keys, second_keys], axis=2)
    live_values = jnp.concatenate([first_values, second_values], axis=2)
    span_cols = TOPK * BLOCK
    live_keys = live_keys.reshape(kv_dev, span_cols, head_dim)
    live_values = live_values.reshape(kv_dev, span_cols, head_dim)
    all_keys = jnp.concatenate([live_keys, prev_keys, stretch_keys], axis=1)
    all_values = jnp.concatenate([live_values, prev_values, stretch_values], axis=1)
    query_rows = queries.reshape(kv_dev, q_per_kv * tok_dev, head_dim)
    step_rows = min(512, q_per_kv * tok_dev)
    columns = jnp.arange(span_cols + 2 * tok_dev, dtype=jnp.int32)

    def one_head(packed):
        q_head, k_head, v_head = packed
        q_steps = q_head.reshape(-1, step_rows, head_dim)
        starts = jnp.arange(q_steps.shape[0], dtype=jnp.int32) * step_rows

        def one_step(packed_block_step):
            q_block, first_row = packed_block_step
            position = (first_row + jnp.arange(step_rows, dtype=jnp.int32)) % tok_dev
            cache_part = columns[None, :] < span_cols
            earlier_part = (
                (columns[None, :] >= span_cols)
                & (columns[None, :] < span_cols + tok_dev)
                & (columns[None, :] - span_cols > position[:, None])
                & (ctx_index > 0)
            )
            own_part = (columns[None, :] >= span_cols + tok_dev) & (
                columns[None, :] - span_cols - tok_dev <= position[:, None]
            )
            return attend(q_block, k_head, v_head, cache_part | earlier_part | own_part)

        return lax.map(one_step, (q_steps, starts)).reshape(q_per_kv * tok_dev, head_dim)

    result = lax.map(one_head, (query_rows, all_keys, all_values))
    return result.reshape(kv_dev * q_per_kv, tok_dev, head_dim)


LOG2E = 1.4426950408889634
MASKED = -1e30
STATS = 8


def rotated(value, axis, by):
    count = lax.axis_size(axis)
    return lax.ppermute(value, axis, [(i, (i + by) % count) for i in range(count)])


def dot(left, right, left_dim, right_dim):
    dims = (((left_dim,), (right_dim,)), ((), ()))
    return lax.dot_general(left, right, dims, preferred_element_type=jnp.float32)


def split_three(row):
    high = row.astype(jnp.bfloat16).astype(jnp.float32)
    rest = row - high
    mid = rest.astype(jnp.bfloat16).astype(jnp.float32)
    return high, mid, rest - mid


def pack_stats(row_max, row_sum):
    parts = split_three(row_max) + split_three(row_sum)
    shape = (STATS, row_max.shape[-1])
    place = lax.broadcasted_iota(jnp.int32, shape, 0)
    packed = jnp.zeros(shape, jnp.float32)
    for index, part in enumerate(parts):
        packed = jnp.where(place == index, jnp.broadcast_to(part, shape), packed)
    return packed


def unpack_stats(packed):
    row_max = packed[0:1] + packed[1:2] + packed[2:3]
    row_sum = packed[3:4] + packed[4:5] + packed[5:6]
    return row_max, row_sum


def soft_parts(score_tiles, value_tiles, unit):
    row_max = functools.reduce(
        jnp.maximum, [jnp.max(tile, axis=0, keepdims=True) for tile in score_tiles]
    )
    row_sum, mixed = 0.0, 0.0
    for scores, values in zip(score_tiles, value_tiles):
        weights = jnp.exp2((scores - row_max) * unit)
        row_sum = row_sum + jnp.sum(weights, axis=0, keepdims=True)
        mixed = mixed + dot(values(), weights.astype(jnp.bfloat16), 0, 0)
    return row_max, row_sum, mixed


def picked(slots_ref, first, count, cache_ref):
    def load(index):
        start = pl.multiple_of(slots_ref[first + index] * BLOCK, BLOCK)
        return cache_ref[0, pl.ds(start, BLOCK), :]

    return [functools.partial(load, index) for index in range(count)]


def first_slot(hop, count, tok_dev, kv_dev, per_peer):
    source = lax.rem(lax.axis_index("ctx") + count - hop, count)
    return (source * tok_dev // BLOCK * kv_dev + pl.program_id(0)) * per_peer


def part_kernel(hop, count, tok_dev, kv_dev, per_peer, step, unit, joined, *refs):
    if joined:
        slots_ref, q_ref, k_ref, v_ref, in_ref, out_ref = refs
    else:
        slots_ref, q_ref, k_ref, v_ref, out_ref = refs
    head_dim = q_ref.shape[-1]
    first = first_slot(hop, count, tok_dev, kv_dev, per_peer)
    keys = picked(slots_ref, first, per_peer, k_ref)
    values = picked(slots_ref, first, per_peer, v_ref)
    for row in range(0, q_ref.shape[0], step):
        rows = slice(row, row + step)
        queries = q_ref[rows, :]
        scores = [dot(load(), queries, 1, 1) for load in keys]
        row_max, row_sum, mixed = soft_parts(scores, values, unit)
        if joined:
            there = in_ref[0, head_dim:, rows].astype(jnp.float32)
            there_max, there_sum = unpack_stats(there)
            top = jnp.maximum(row_max, there_max)
            here_by = jnp.exp2((row_max - top) * unit)
            there_sum = there_sum * jnp.exp2((there_max - top) * unit)
            there_mixed = in_ref[0, :head_dim, rows].astype(jnp.float32)
            row_max, row_sum = top, row_sum * here_by + there_sum
            mixed = mixed * here_by + there_mixed * there_sum
        out_ref[0, :head_dim, rows] = (mixed * (1.0 / row_sum)).astype(out_ref.dtype)
        out_ref[0, head_dim:, rows] = pack_stats(row_max, row_sum).astype(out_ref.dtype)


def own_kernel(
    count, tok_dev, kv_dev, per_peer, step, unit, slots_ref, q_ref, k_ref, v_ref,
    near_k_ref, near_v_ref, prev_ref, mixed_ref, stats_ref,
):
    head_dim = q_ref.shape[-1]
    first = first_slot(0, count, tok_dev, kv_dev, per_peer)
    keys = picked(slots_ref, first, per_peer, k_ref)
    values = picked(slots_ref, first, per_peer, v_ref)
    keys += [lambda: prev_ref[0, 0], lambda: near_k_ref[0]]
    values += [lambda: prev_ref[1, 0], lambda: near_v_ref[0]]
    shape = (tok_dev, step)
    place = lax.broadcasted_iota(jnp.int32, shape, 0)
    position = lax.broadcasted_iota(jnp.int32, shape, 1) % tok_dev
    held = place <= position
    before = (place > position) & (lax.axis_index("ctx") > 0)
    for row in range(0, q_ref.shape[0], step):
        rows = slice(row, row + step)
        queries = q_ref[rows, :]
        scores = [dot(load(), queries, 1, 1) for load in keys]
        scores[-2] = jnp.where(before, scores[-2], MASKED)
        scores[-1] = jnp.where(held, scores[-1], MASKED)
        row_max, row_sum, mixed = soft_parts(scores, values, unit)
        mixed_ref[0, :, rows] = mixed
        where = lax.broadcasted_iota(jnp.int32, (STATS, step), 0)
        stats_ref[0, :, rows] = jnp.where(where == 0, row_max, row_sum)


def join_kernel(unit, mixed_ref, stats_ref, left_ref, right_ref, out_ref):
    head_dim, step = mixed_ref.shape[1], out_ref.shape[1]
    for index in range(out_ref.shape[0]):
        rows = slice(index * step, (index + 1) * step)
        stats = stats_ref[0, :, rows]
        own_max, own_sum = stats[0:1], stats[1:2]
        left_max, left_sum = unpack_stats(left_ref[0, head_dim:, rows].astype(jnp.float32))
        right_max, right_sum = unpack_stats(right_ref[0, head_dim:, rows].astype(jnp.float32))
        top = jnp.maximum(own_max, jnp.maximum(left_max, right_max))
        own_by = jnp.exp2((own_max - top) * unit)
        left_by = jnp.exp2((left_max - top) * unit) * left_sum
        right_by = jnp.exp2((right_max - top) * unit) * right_sum
        share = 1.0 / (own_sum * own_by + left_by + right_by)
        mixed = mixed_ref[0, :, rows] * (own_by * share)
        mixed += left_ref[0, :head_dim, rows].astype(jnp.float32) * (left_by * share)
        mixed += right_ref[0, :head_dim, rows].astype(jnp.float32) * (right_by * share)
        out_ref[index] = jnp.transpose(mixed).astype(out_ref.dtype)


def moved_queries(
    queries, stretch_keys, stretch_values, cache_keys, cache_values, block_picks, block_table
):
    kv_dev, tok_dev, head_dim = stretch_keys.shape
    q_per_kv = queries.shape[0] // kv_dev
    cache_rows = cache_keys.shape[1]
    blocks_dev = cache_rows // BLOCK
    count = lax.axis_size("ctx")
    ctx_index = lax.axis_index("ctx")
    per_peer = TOPK // count
    rows = q_per_kv * tok_dev
    step = min(512, rows)
    unit = head_dim**-0.5 * LOG2E
    flat = queries.reshape(kv_dev * rows, head_dim)
    around = {0: flat}
    for hop in range(1, count):
        around[hop] = rotated(around[hop - 1], "ctx", 1)
    prev = shifted(jnp.stack([stretch_keys, stretch_values]), "ctx", 1)

    head_ids = lax.axis_index(("head", "tp")) * kv_dev + jnp.arange(kv_dev, dtype=jnp.int32)
    selector = head_ids[:, None] == jnp.arange(block_picks.shape[1], dtype=jnp.int32)[None, :]
    my_picks = jnp.sum(jnp.where(selector[None, :, :, None], block_picks[:, None, :, :], 0), axis=2)
    physical = lookup(block_table, my_picks)
    mine = physical // blocks_dev == ctx_index
    rank = jnp.cumsum(mine.astype(jnp.int32), axis=-1) - 1
    slot_ids = jnp.arange(per_peer, dtype=jnp.int32)
    matched = mine[..., None, :] & (rank[..., None, :] == slot_ids[:, None])
    slots = jnp.sum(jnp.where(matched, (physical % blocks_dev)[..., None, :], 0), axis=-1)
    slots = slots.reshape(-1)

    q_spec = pl.BlockSpec((rows, head_dim), lambda h, s: (h, 0))
    cache_spec = pl.BlockSpec((1, cache_rows, head_dim), lambda h, s: (h, 0, 0))
    near_spec = pl.BlockSpec((1, tok_dev, head_dim), lambda h, s: (h, 0, 0))
    prev_spec = pl.BlockSpec((2, 1, tok_dev, head_dim), lambda h, s: (0, h, 0, 0))
    part_spec = pl.BlockSpec((1, head_dim + STATS, rows), lambda h, s: (h, 0, 0))
    part_shape = jax.ShapeDtypeStruct((kv_dev, head_dim + STATS, rows), jnp.bfloat16)
    params = pltpu.CompilerParams(vmem_limit_bytes=48 << 20)

    def cost(columns):
        pairs = kv_dev * rows * columns
        return pl.CostEstimate(
            flops=8 * pairs * head_dim, bytes_accessed=8 << 20, transcendentals=pairs
        )

    def part(hop, given):
        body = functools.partial(
            part_kernel, hop, count, tok_dev, kv_dev, per_peer, step, unit, given is not None
        )
        extra = [] if given is None else [given]
        return pl.pallas_call(
            body,
            out_shape=part_shape,
            grid_spec=pltpu.PrefetchScalarGridSpec(
                num_scalar_prefetch=1,
                grid=(kv_dev,),
                in_specs=[q_spec, cache_spec, cache_spec] + [part_spec] * len(extra),
                out_specs=part_spec,
            ),
            compiler_params=params,
            cost_estimate=cost(per_peer * BLOCK),
            name=f"part{hop}",
        )(slots, around[hop], cache_keys, cache_values, *extra)

    left = rotated(part(1, None), "ctx", -1)
    right = None
    for hop in range(2, count):
        right = rotated(part(hop, right), "ctx", 1)

    mixed_shape = jax.ShapeDtypeStruct((kv_dev, head_dim, rows), jnp.float32)
    stats_shape = jax.ShapeDtypeStruct((kv_dev, STATS, rows), jnp.float32)
    mixed_spec = pl.BlockSpec((1, head_dim, rows), lambda h, *s: (h, 0, 0))
    stats_spec = pl.BlockSpec((1, STATS, rows), lambda h, *s: (h, 0, 0))
    mixed, stats = pl.pallas_call(
        functools.partial(own_kernel, count, tok_dev, kv_dev, per_peer, step, unit),
        out_shape=(mixed_shape, stats_shape),
        grid_spec=pltpu.PrefetchScalarGridSpec(
            num_scalar_prefetch=1,
            grid=(kv_dev,),
            in_specs=[q_spec, cache_spec, cache_spec, near_spec, near_spec, prev_spec],
            out_specs=(mixed_spec, stats_spec),
        ),
        compiler_params=params,
        cost_estimate=cost(per_peer * BLOCK + 2 * tok_dev),
        name="own",
    )(slots, flat, cache_keys, cache_values, stretch_keys, stretch_values, prev)

    joined_spec = pl.BlockSpec((1, head_dim + STATS, rows), lambda h: (h, 0, 0))
    return pl.pallas_call(
        functools.partial(join_kernel, unit),
        out_shape=jax.ShapeDtypeStruct(queries.shape, queries.dtype),
        grid=(kv_dev,),
        in_specs=[mixed_spec, stats_spec, joined_spec, joined_spec],
        out_specs=pl.BlockSpec((q_per_kv, tok_dev, head_dim), lambda h: (h, 0, 0)),
        compiler_params=params,
        name="join",
    )(mixed, stats, left, right)


def shards(count, *arrays):
    if count > 2 and TOPK % count == 0 and count <= 8:
        return moved_queries(*arrays)
    return moved_blocks(*arrays)


def solution(mesh):
    placed = (
        P(("head", "tp"), ("groups", "ctx"), None),
        P(("head", "tp"), ("groups", "ctx"), None),
        P(("head", "tp"), ("groups", "ctx"), None),
        P(("head", "tp"), ("groups", "ctx"), None),
        P(("head", "tp"), ("groups", "ctx"), None),
        P("groups", None, None),
        P("groups"),
    )
    return jax.shard_map(
        functools.partial(shards, mesh.shape["ctx"]),
        mesh=mesh,
        in_specs=placed,
        out_specs=P(("head", "tp"), ("groups", "ctx"), None),
        check_vma=False,
    )
```
